512 devices in a mesh: dp: 16 (over y, core), seq: 32 (over x, z).
Axes of the slice: x: 4, y: 8, z: 8, core: 2. Of those that a mesh axis runs over, the one named last changes fastest.
Arguments:
- queries: bfloat16 [131072, 4096], P(('dp', 'seq')), parts along dimension 0, may hold values from -6 to 6
- keys: bfloat16 [131072, 1024], P(('dp', 'seq')), parts along dimension 0, may hold values from -6 to 6
- values: bfloat16 [131072, 1024], P(('dp', 'seq')), parts along dimension 0, may hold values from -6 to 6
- lengths: int32 [512], P('dp'), parts along dimension 0, may hold values from 1 to 1024, 8192 in all
- span_order: int32 [2048], P('dp'), parts along dimension 0, may hold values from 0 to 127, each once
Outputs:
- attended: bfloat16 [131072, 4096], P(('dp', 'seq')), parts along dimension 0
The draws below stay inside these ranges and needn't reach their ends.
There are 16 independent parts, one for each index of `dp`. The reference program is written for one: setup_inputs(seed, part) draws one part's arguments, and reference() takes and returns one part's arrays. A program takes and returns all parts, laid end to end along the dimension named above; each array names one. Nothing has to cross between parts.
Inputs may be any that keep to these rules, and one draw needn't show every extreme that they name: The lengths of one packed sequence sum to 8192; the longest is exactly 1024. A permutation of the 128 spans: balanced row b * 64 + i holds loader token span_order[b] * 64 + i.
All inputs are finite; a program needn't handle non-finite values.
Results may differ from the reference program's by a relative error of at most 0.0034.
Values may be sent and summed in bfloat16 or wider, within the bound.
A program may use at most 64 MiB of HBM per device.

```python
import math
import jax
import jax.numpy as jnp
import numpy as np
from jax import lax

HEADS = 32
KV_HEADS = 8
HEAD_DIM = 128
BLOCK = 64
DOC_MOST = 1024
QBLOCK = 512
TOKENS = 8192
NDOC = 32
NCHUNK = 128


def draw_queries(key, part):
    width = HEADS * HEAD_DIM
    drawn = jnp.clip(jax.random.normal(jax.random.fold_in(key, 1), (TOKENS, width), jnp.float32), -4.0, 4.0)
    return drawn.astype(jnp.bfloat16)


def draw_keys(key, part):
    width = KV_HEADS * HEAD_DIM
    drawn = jnp.clip(jax.random.normal(jax.random.fold_in(key, 2), (TOKENS, width), jnp.float32), -4.0, 4.0)
    return drawn.astype(jnp.bfloat16)


def steps_of(stream_key, extent, cuts, least, top_value):
    def one(axis_at, blocks):
        steps = jax.random.uniform(jax.random.fold_in(jax.random.fold_in(stream_key, 6), axis_at), (blocks,), jnp.float32, least / len(cuts), top_value / len(cuts))
        return jnp.repeat(jnp.exp(steps), extent[axis_at] // blocks).reshape((-1,) + (1,) * (len(extent) - axis_at - 1))

    level = one(*cuts[0])
    for cut in cuts[1:]:
        level = level * one(*cut)
    return level


def split_up(number_of, total, limit, skew):
    weights = [(1 << 20) // math.isqrt(rank ** skew) + 1 for rank in range(2, number_of + 1)]
    surplus, counts = total - limit - (number_of - 1), [1] * (number_of - 1)
    while surplus > 0:
        movable = [i for i in range(number_of - 1) if counts[i] < limit]
        pool, remaining = sum([weights[i] for i in movable]), surplus
        for i in movable:
            addition = min(limit - counts[i], max(1, remaining * weights[i] // pool), surplus)
            counts[i] = counts[i] + addition
            surplus = surplus - addition
    return np.array([limit] + counts)


def ragged(key, number_of, total, limit, lean):
    if number_of == 2:
        one = jax.random.randint(key, (), max(1, total - limit), min(limit, total - 1) + 1)
        return jnp.stack([one, total - one])
    tallies = jnp.asarray(split_up(number_of, total, limit, lean), jnp.int32)
    couples = (number_of - 1) // 2
    donor, receiver = tallies[1:1 + 2 * couples:2], tallies[2:2 + 2 * couples:2]
    room = jnp.minimum(donor - 1, limit - receiver)
    passed = jax.random.randint(jax.random.fold_in(key, 1), (couples,), 0, 1 << 20) % (room + 1)
    tallies = tallies.at[1:1 + 2 * couples:2].set(donor - passed).at[2:2 + 2 * couples:2].set(receiver + passed)
    return tallies[jax.random.permutation(jax.random.fold_in(key, 2), number_of)]


def gaussian(stream_key, shape, spread, reach, shards=(), kind=jnp.bfloat16):
    entries = spread * jax.random.normal(stream_key, shape, jnp.float32)
    if shards:
        entries = entries * steps_of(stream_key, shape, shards, -0.22, 0.18)
    return jnp.clip(entries, -reach, reach).astype(kind)


def setup_inputs(seed: int = 0, part: int = 0) -> dict:
    seeds = jax.random.split(jax.random.key(seed), 6)
    own_keys = jax.random.split(jax.random.fold_in(seeds[5], part), 6)
    queries = draw_queries(jax.random.fold_in(jax.random.fold_in(seeds[5], part), 71), part)
    keys = draw_keys(jax.random.fold_in(jax.random.fold_in(seeds[5], part), 71), part)
    values = gaussian(own_keys[2], (TOKENS, KV_HEADS * HEAD_DIM), 1.0, 6.0, ((0, 32),))
    lengths = ragged(own_keys[3], NDOC, TOKENS, DOC_MOST, 1).astype(jnp.int32)
    span_order = jax.random.permutation(own_keys[4], NCHUNK).astype(jnp.int32)
    return {"queries": queries, "keys": keys, "values": values, "lengths": lengths, "span_order": span_order}


def doc_numbers(lengths, places):
    doc_ends = jnp.cumsum(lengths.astype(jnp.int32))
    return jnp.sum((doc_ends[None, :] <= places[:, None]).astype(jnp.int32), axis=1)


def band_attention(query_group, key_rows, value_rows, doc_ids):
    total_rows = query_group.shape[0]
    group_size = query_group.shape[1]
    pad_keys = jnp.concatenate([jnp.zeros((DOC_MOST, HEAD_DIM), key_rows.dtype), key_rows], 0)
    pad_values = jnp.concatenate([jnp.zeros((DOC_MOST, HEAD_DIM), value_rows.dtype), value_rows], 0)
    pad_docs = jnp.concatenate([jnp.full((DOC_MOST,), -1, jnp.int32), doc_ids.astype(jnp.int32)], 0)
    scale_factor = HEAD_DIM ** -0.5

    def one_block(block_index):
        row_start = (block_index * QBLOCK).astype(jnp.int32)
        query_block = lax.dynamic_slice_in_dim(query_group, row_start, QBLOCK, 0)
        key_block = lax.dynamic_slice_in_dim(pad_keys, row_start, QBLOCK + DOC_MOST, 0)
        value_block = lax.dynamic_slice_in_dim(pad_values, row_start, QBLOCK + DOC_MOST, 0)
        query_docs = lax.dynamic_slice_in_dim(pad_docs, row_start + DOC_MOST, QBLOCK, 0)
        key_docs = lax.dynamic_slice_in_dim(pad_docs, row_start, QBLOCK + DOC_MOST, 0)
        query_pos = row_start + jnp.arange(QBLOCK, dtype=jnp.int32)
        key_pos = row_start - DOC_MOST + jnp.arange(QBLOCK + DOC_MOST, dtype=jnp.int32)
        allowed = (query_docs[:, None] == key_docs[None, :]) & (key_pos[None, :] <= query_pos[:, None])
        scores = jnp.einsum("qgd,kd->gqk", query_block.astype(jnp.float32), key_block.astype(jnp.float32)) * scale_factor
        scores = jnp.where(allowed[None], scores, -jnp.inf)
        row_top = jnp.max(scores, axis=-1, keepdims=True)
        weights = jnp.exp(scores - row_top)
        row_total = jnp.sum(weights, axis=-1, keepdims=True)
        rounded = lax.optimization_barrier(weights.astype(jnp.bfloat16))
        mixed_rows = jnp.einsum("gqk,kd->qgd", rounded.astype(jnp.float32), value_block.astype(jnp.float32))
        return (mixed_rows / jnp.transpose(row_total, (1, 0, 2))).astype(jnp.bfloat16)

    blocks = lax.map(one_block, jnp.arange(total_rows // QBLOCK, dtype=jnp.int32))
    return blocks.reshape(total_rows, group_size * HEAD_DIM)


def reference(queries, keys, values, lengths, span_order):
    total_rows = queries.shape[0]
    nchunk = span_order.shape[0]
    inverse = jnp.zeros((nchunk,), jnp.int32).at[span_order].set(jnp.arange(nchunk, dtype=jnp.int32))
    places = jnp.arange(total_rows, dtype=jnp.int32)
    doc_ids = doc_numbers(lengths, places)

    def to_loader(array):
        return array.reshape(nchunk, BLOCK, -1)[inverse].reshape(total_rows, -1)

    loader_queries = to_loader(queries)
    loader_keys = to_loader(keys)
    loader_values = to_loader(values)
    group_size = HEADS // KV_HEADS

    def per_kv(kv_index):
        query_group = lax.dynamic_slice_in_dim(loader_queries, kv_index * group_size * HEAD_DIM, group_size * HEAD_DIM, 1)
        query_group = query_group.reshape(total_rows, group_size, HEAD_DIM)
        key_rows = lax.dynamic_slice_in_dim(loader_keys, kv_index * HEAD_DIM, HEAD_DIM, 1)
        value_rows = lax.dynamic_slice_in_dim(loader_values, kv_index * HEAD_DIM, HEAD_DIM, 1)
        return band_attention(query_group, key_rows, value_rows, doc_ids)

    group_outputs = lax.map(per_kv, jnp.arange(KV_HEADS, dtype=jnp.int32))
    loader_out = jnp.transpose(group_outputs, (1, 0, 2)).reshape(total_rows, HEADS * HEAD_DIM)
    return loader_out.reshape(nchunk, BLOCK, -1)[span_order].reshape(total_rows, -1)
```

```python
import math

import jax
import jax.numpy as jnp
from jax import lax
from jax.experimental import pallas as pl
from jax.experimental.pallas import tpu as pltpu
from jax.sharding import PartitionSpec as P

HEADS = 32
KV_HEADS = 8
HEAD_DIM = 128
BLOCK = 64
NX = 4
NZ = 8
ROWS = 256
SPANS = ROWS // BLOCK
GROUP = HEADS // KV_HEADS
KVH = KV_HEADS // NX
QW = HEADS * HEAD_DIM // NX
GW = GROUP * HEAD_DIM
TOKENS = NX * NZ * ROWS
NSPAN = TOKENS // BLOCK
PAD = 17
WIN = 18
UNITS = NX * SPANS
HALF = UNITS // 2
NDOC = 32
FORWARDS = 10
SCALE = HEAD_DIM**-0.5 * math.log2(math.e)


def body(
    lengths, order, places, queries, keys, values, out,
    kv_first, kv_second, loader_k, loader_v, q_buf, o_buf, starts,
    x_send, x_recv, q_send, q_recv, z_send, z_recv, o_send, o_recv,
):
    me = lax.axis_index("seq")
    x = me // NZ
    z = lax.rem(me, NZ)

    def at_x(offset):
        return lax.rem(x + offset, NX)

    def at_z(offset):
        return lax.rem(z + offset + NZ, NZ)

    def seq_of(xx, zz):
        return {"seq": xx * NZ + zz}

    barrier = pltpu.get_barrier_semaphore()
    partners = [seq_of(at_x(d), z) for d in range(1, NX)]
    partners += [seq_of(x, at_z(1)), seq_of(x, at_z(-1))]
    for partner in partners:
        pl.semaphore_signal(barrier, inc=1, device_id=partner, device_id_type=pl.DeviceIdType.MESH)
    pl.semaphore_wait(barrier, len(partners))

    kv = (kv_first, kv_second)

    def kv_rows(h, item, zz, xx):
        return kv[h].at[item, pl.ds(zz * UNITS + xx * SPANS, SPANS)]

    def kv_source(h, item, xx):
        source = (keys, values)[item]
        first = pl.multiple_of(xx * (KVH * HEAD_DIM) + h * HEAD_DIM, HEAD_DIM)
        return source.at[:, :, pl.ds(first, HEAD_DIM)]

    def x_copy(h, item, d):
        return pltpu.make_async_remote_copy(
            src_ref=kv_source(h, item, at_x(d)),
            dst_ref=kv_rows(h, item, z, x),
            send_sem=x_send.at[h, item, d - 1],
            recv_sem=x_recv.at[h, item, x],
            device_id=seq_of(at_x(d), z),
            device_id_type=pl.DeviceIdType.MESH,
        )

    def x_own(h, item):
        return pltpu.make_async_copy(
            kv_source(h, item, x), kv_rows(h, item, z, x), x_recv.at[h, item, x]
        )

    def q_source(h, xx):
        return queries.at[:, pl.ds(pl.multiple_of(xx * QW + h * GW, GW), GW)]

    def q_copy(h, d):
        return pltpu.make_async_remote_copy(
            src_ref=q_source(h, at_x(d)),
            dst_ref=q_buf.at[h, x],
            send_sem=q_send.at[h, d - 1],
            recv_sem=q_recv.at[h, x],
            device_id=seq_of(at_x(d), z),
            device_id_type=pl.DeviceIdType.MESH,
        )

    def q_own(h):
        return pltpu.make_async_copy(q_source(h, x), q_buf.at[h, x], q_recv.at[h, x])

    for h in range(KVH):
        for item in range(2):
            for d in (2, 1, 3):
                x_copy(h, item, d).start()
            x_own(h, item).start()
    for h in range(KVH):
        for d in (2, 1, 3):
            q_copy(h, d).start()
        q_own(h).start()

    def piece(h, item, half, zz):
        return kv[h].at[item, pl.ds(zz * UNITS + half * HALF, HALF)]

    def z_copy(h, way, hop, item, half):
        turn = 1 - 2 * way
        ref = piece(h, item, half, at_z(-turn * (hop - 1)))
        return pltpu.make_async_remote_copy(
            src_ref=ref,
            dst_ref=ref,
            send_sem=z_send.at[h, way, hop - 1, item, half],
            recv_sem=z_recv.at[h, way, hop - 1, item, half],
            device_id=seq_of(x, at_z(turn)),
            device_id_type=pl.DeviceIdType.MESH,
        )

    def z_arrived(h, way, hop, item, half):
        turn = 1 - 2 * way
        ref = piece(h, item, half, at_z(-turn * hop))
        pltpu.make_async_copy(ref, ref, z_recv.at[h, way, hop - 1, item, half]).wait()

    def z_first(h):
        for item in range(2):
            for half in range(2):
                for xx in (2 * half, 2 * half + 1):
                    ref = kv_rows(h, item, z, xx)
                    pltpu.make_async_copy(ref, ref, x_recv.at[h, item, xx]).wait()
                for way in range(2):
                    z_copy(h, way, 1, item, half).start()

    def z_forward(h, e):
        late = e // 8
        hop = 1 + e // 4
        item = (1 - late) * ((e % 4) // 2) + late * (e % 2)
        for way in range(2):
            half = (1 - late) * (e % 2) + late * way
            z_arrived(h, way, hop, item, half)
            z_copy(h, way, hop + 1, item, half).start()

    def z_last(h):
        for item in range(2):
            for way in range(2):
                z_arrived(h, way, 3, item, 1 - way)
        for item in range(2):
            for way in range(2):
                z_arrived(h, way, 4, item, way)

    def unit_of(u):
        d = lax.rem(lax.rem(u, NX) + 1, NX)
        return d, u // NX

    def span_of(u):
        d, s = unit_of(u)
        return order[(at_x(d) * NZ + z) * SPANS + s]

    z_first(0)

    def find_starts(u, carry):
        span = span_of(u)
        token = span * BLOCK + lax.broadcasted_iota(jnp.int32, (BLOCK, HEAD_DIM), 0)
        start = jnp.zeros((BLOCK, HEAD_DIM), jnp.int32)
        end = jnp.int32(0)
        for j in range(NDOC):
            end = end + lengths[j]
            start = jnp.where(token >= end, end, start)
        starts[u] = start - (span - PAD) * BLOCK
        return carry

    lax.fori_loop(0, UNITS, find_starts, 0)
    loader_k[0:PAD] = jnp.zeros((PAD, BLOCK, HEAD_DIM), jnp.bfloat16)
    loader_v[0:PAD] = jnp.zeros((PAD, BLOCK, HEAD_DIM), jnp.bfloat16)

    def forward_step(e, carry):
        z_forward(0, e)
        return carry

    lax.fori_loop(0, FORWARDS, forward_step, 0)
    z_first(1)

    for h in range(KVH):
        for xx in range(NX):
            pltpu.make_async_copy(q_buf.at[h, xx], q_buf.at[h, xx], q_recv.at[h, xx]).wait()

    lane = lax.broadcasted_iota(jnp.int32, (GROUP * BLOCK, 128), 1)
    row = lax.rem(lax.broadcasted_iota(jnp.int32, (GROUP * BLOCK, 128), 0), BLOCK)

    def o_rows(s, h, xx):
        return out.at[
            pl.ds(pl.multiple_of(s * BLOCK, BLOCK), BLOCK),
            pl.ds(pl.multiple_of(xx * QW + h * GW, GW), GW),
        ]

    def o_source(h, d, s):
        return o_buf.at[h, d, pl.ds(pl.multiple_of(s * BLOCK, BLOCK), BLOCK), :]

    def o_copy(h, d, s):
        return pltpu.make_async_remote_copy(
            src_ref=o_source(h, d, s),
            dst_ref=o_rows(s, h, x),
            send_sem=o_send.at[h, d, s],
            recv_sem=o_recv.at[h, d, s],
            device_id=seq_of(at_x(d), z),
            device_id_type=pl.DeviceIdType.MESH,
        )

    def o_own(h, s):
        return pltpu.make_async_copy(o_source(h, 0, s), o_rows(s, h, x), o_recv.at[h, 0, s])

    def send_unit(h, u):
        d, s = unit_of(u)

        @pl.when(d > 0)
        def _():
            o_copy(h, d, s).start()

        @pl.when(d == 0)
        def _():
            o_own(h, s).start()

    def attend(h, u):
        d, s = unit_of(u)
        xx = at_x(d)
        first = pl.multiple_of(s * BLOCK, BLOCK)
        q_rows = q_buf[h, xx, pl.ds(first, BLOCK), :]
        q = jnp.concatenate([q_rows[:, g * HEAD_DIM : (g + 1) * HEAD_DIM] for g in range(GROUP)], 0)
        span = span_of(u)
        window_k = jnp.concatenate([loader_k[span + n] for n in range(WIN)], 0)
        window_v = jnp.concatenate([loader_v[span + n] for n in range(WIN)], 0)
        scores = lax.dot_general(
            q, window_k, (((1,), (1,)), ((), ())), preferred_element_type=jnp.float32
        )
        start = starts[u]
        start = jnp.concatenate([start] * GROUP, 0)
        parts = []
        for c in range(WIN // 2):
            allowed = lane >= start - 128 * c
            if c == WIN // 2 - 1:
                allowed = allowed & (lane - BLOCK <= row)
            parts.append(jnp.where(allowed, scores[:, c * 128 : (c + 1) * 128], -jnp.inf))
        top = parts[0]
        for part in parts[1:]:
            top = jnp.maximum(top, part)
        top = jnp.max(top, axis=1, keepdims=True)
        parts = [jnp.exp2((part - top) * SCALE) for part in parts]
        total = parts[0]
        for part in parts[1:]:
            total = total + part
        total = jnp.sum(total, axis=1, keepdims=True)
        rounded = jnp.concatenate([part.astype(jnp.bfloat16) for part in parts], 1)
        mixed = jnp.dot(rounded, window_v, preferred_element_type=jnp.float32)
        mixed = (mixed / total).astype(jnp.bfloat16)
        for g in range(GROUP):
            o_buf[h, d, pl.ds(first, BLOCK), g * HEAD_DIM : (g + 1) * HEAD_DIM] = mixed[
                g * BLOCK : (g + 1) * BLOCK
            ]

    def to_loader(h):
        def move(i, carry):
            for n in range(4):
                t = 4 * i + n
                loader_k[PAD + t] = kv[h][0, places[t]]
                loader_v[PAD + t] = kv[h][1, places[t]]
            return carry

        lax.fori_loop(0, NSPAN // 4, move, 0)

    for h in range(KVH):
        z_last(h)
        to_loader(h)

        def unit_step(u, carry):
            if h == 0:

                @pl.when(u < FORWARDS)
                def _():
                    z_forward(1, u)

            attend(h, u)

            @pl.when(u > 0)
            def _():
                send_unit(h, u - 1)

            return carry

        lax.fori_loop(0, UNITS, unit_step, 0)
        send_unit(h, UNITS - 1)

    for h in range(KVH):
        for s in range(SPANS):
            o_own(h, s).wait()
            for d in range(1, NX):
                o_copy(h, d, s).wait_send()
                ref = o_rows(s, h, at_x(NX - d))
                pltpu.make_async_copy(ref, ref, o_recv.at[h, d, s]).wait()
    for h in range(KVH):
        for d in range(1, NX):
            for item in range(2):
                x_copy(h, item, d).wait_send()
            q_copy(h, d).wait_send()
        for item in range(2):
            for way in range(2):
                for half in range(2):
                    for hop in range(1, 5 if half == way else 4):
                        z_copy(h, way, hop, item, half).wait_send()


def shards(queries, keys, values, lengths, span_order):
    spans = jnp.arange(NSPAN, dtype=jnp.int32)
    holder = spans // SPANS
    place = ((holder % NZ) * NX + holder // NZ) * SPANS + spans % SPANS
    places = jnp.sum(jnp.where(span_order[:, None] == spans[None, :], place[:, None], 0), axis=0)
    smem = pl.BlockSpec(memory_space=pltpu.SMEM)
    anywhere = pl.BlockSpec(memory_space=pl.ANY)
    dma = pltpu.SemaphoreType.DMA
    return pl.pallas_call(
        body,
        out_shape=jax.ShapeDtypeStruct((ROWS, HEADS * HEAD_DIM), jnp.bfloat16),
        in_specs=[smem, smem, smem, anywhere, anywhere, anywhere],
        out_specs=anywhere,
        scratch_shapes=[
            pltpu.VMEM((2, NSPAN, BLOCK, HEAD_DIM), jnp.bfloat16),
            pltpu.VMEM((2, NSPAN, BLOCK, HEAD_DIM), jnp.bfloat16),
            pltpu.VMEM((PAD + NSPAN, BLOCK, HEAD_DIM), jnp.bfloat16),
            pltpu.VMEM((PAD + NSPAN, BLOCK, HEAD_DIM), jnp.bfloat16),
            pltpu.VMEM((KVH, NX, ROWS, GW), jnp.bfloat16),
            pltpu.VMEM((KVH, NX, ROWS, GW), jnp.bfloat16),
            pltpu.VMEM((UNITS, BLOCK, HEAD_DIM), jnp.int32),
            dma((KVH, 2, NX - 1)),
            dma((KVH, 2, NX)),
            dma((KVH, NX - 1)),
            dma((KVH, NX)),
            dma((KVH, 2, 4, 2, 2)),
            dma((KVH, 2, 4, 2, 2)),
            dma((KVH, NX, SPANS)),
            dma((KVH, NX, SPANS)),
        ],
        compiler_params=pltpu.CompilerParams(collective_id=0, has_side_effects=True),
        name="span_attention",
    )(
        lengths, span_order, places.astype(jnp.int32), queries,
        keys.reshape(SPANS, BLOCK, KV_HEADS * HEAD_DIM),
        values.reshape(SPANS, BLOCK, KV_HEADS * HEAD_DIM),
    )


def solution(mesh):
    placed = (
        P(("dp", "seq"), None),
        P(("dp", "seq"), None),
        P(("dp", "seq"), None),
        P("dp"),
        P("dp"),
    )
    return jax.shard_map(
        shards, mesh=mesh, in_specs=placed, out_specs=P(("dp", "seq"), None), check_vma=False
    )
```

```python
import functools
import math

import jax
import jax.numpy as jnp
from jax import lax
from jax.experimental import pallas as pl
from jax.experimental.pallas import tpu as pltpu
from jax.sharding import PartitionSpec as P

HEADS = 32
KV_HEADS = 8
HEAD_DIM = 128
BLOCK = 64
NX = 4
NZ = 8
ROWS = 256
SPANS = ROWS // BLOCK
GROUP = HEADS // KV_HEADS
KVH = KV_HEADS // NX
QW = HEADS * HEAD_DIM // NX
GW = GROUP * HEAD_DIM
TOKENS = NX * NZ * ROWS
NSPAN = TOKENS // BLOCK
PAD = 17
WIN = 18
UNITS = NX * SPANS
HALF = UNITS // 2
NDOC = 32
SCALE = HEAD_DIM**-0.5 * math.log2(math.e)


def body(
    lengths, order, places, queries, keys, values, out,
    k_first, v_first, k_second, v_second, q_buf, o_buf, starts, scores, weights, totals,
    x_send, x_recv, q_send, q_recv, z_send, z_recv, o_send, o_recv,
):
    me = lax.axis_index("seq")
    x = me // NZ
    z = lax.rem(me, NZ)
    kv = ((k_first, v_first), (k_second, v_second))

    def at_x(offset):
        return lax.rem(x + offset, NX)

    def at_z(offset):
        return lax.rem(z + offset + NZ, NZ)

    def seq_of(xx, zz):
        return {"seq": xx * NZ + zz}

    def send(src_ref, dst_ref, send_sem, recv_sem, target):
        return pltpu.make_async_remote_copy(
            src_ref=src_ref,
            dst_ref=dst_ref,
            send_sem=send_sem,
            recv_sem=recv_sem,
            device_id=target,
            device_id_type=pl.DeviceIdType.MESH,
        )

    def arrived(ref, sem):
        pltpu.make_async_copy(ref, ref, sem).wait()

    barrier = pltpu.get_barrier_semaphore()
    partners = [seq_of(at_x(d), z) for d in range(1, NX)]
    partners += [seq_of(x, at_z(1)), seq_of(x, at_z(-1))]
    for partner in partners:
        pl.semaphore_signal(barrier, inc=1, device_id=partner, device_id_type=pl.DeviceIdType.MESH)
    pl.semaphore_wait(barrier, len(partners))

    def kv_rows(h, item, d):
        return kv[h][item].at[pl.ds(z * UNITS + d * SPANS, SPANS)]

    def kv_source(h, item, d):
        first = pl.multiple_of(at_x(d) * (KVH * HEAD_DIM) + h * HEAD_DIM, HEAD_DIM)
        return (keys, values)[item].at[:, :, pl.ds(first, HEAD_DIM)]

    def x_copy(h, item, d):
        source, target, sem = kv_source(h, item, d), kv_rows(h, item, d), x_recv.at[h, item, d]
        if d == 0:
            return pltpu.make_async_copy(source, target, sem)
        return send(source, target, x_send.at[h, item, d], sem, seq_of(at_x(d), z))

    def q_copy(h, d):
        source = queries.at[:, pl.ds(pl.multiple_of(at_x(d) * QW + h * GW, GW), GW)]
        target, sem = q_buf.at[h, d], q_recv.at[h, d]
        if d == 0:
            return pltpu.make_async_copy(source, target, sem)
        return send(source, target, q_send.at[h, d], sem, seq_of(at_x(d), z))

    for h in range(KVH):
        for item in range(2):
            for d in range(NX):
                x_copy(h, item, d).start()
        for d in range(NX):
            q_copy(h, d).start()

    def piece(h, item, half, zz):
        return kv[h][item].at[pl.ds(zz * UNITS + half * HALF, HALF)]

    def z_copy(h, item, way, hop, half):
        turn = 1 - 2 * way
        ref = piece(h, item, half, at_z(-turn * (hop - 1)))
        sems = (h, item, way, hop - 1, half)
        return send(ref, ref, z_send.at[sems], z_recv.at[sems], seq_of(x, at_z(turn)))

    def z_arrived(h, item, way, hop, half):
        ref = piece(h, item, half, at_z((2 * way - 1) * hop))
        arrived(ref, z_recv.at[h, item, way, hop - 1, half])

    def z_start(h, item):
        for half in range(2):
            for d in (2 * half, 2 * half + 1):
                arrived(kv_rows(h, item, d), x_recv.at[h, item, d])
            for way in range(2):
                z_copy(h, item, way, 1, half).start()

    def z_forward(h, item, hop, half):
        for way in range(2):
            part = half if hop < 4 else way
            z_arrived(h, item, way, hop - 1, part)
            z_copy(h, item, way, hop, part).start()

    def z_forward_both(h, item, hop):
        for half in range(2):
            z_forward(h, item, hop, half)

    def z_finish(h, item):
        for way in range(2):
            z_arrived(h, item, way, 3, 1 - way)
        for way in range(2):
            z_arrived(h, item, way, 4, way)

    def unit_of(u):
        d = lax.rem(lax.rem(u, NX) + 1, NX)
        return d, u // NX

    def span_of(u):
        d, s = unit_of(u)
        return order[(at_x(d) * NZ + z) * SPANS + s]

    def run_units(step, events=()):
        def unit_step(u, carry):
            for when, event in events:
                pl.when(u == when)(event)
            step(u)
            return carry

        lax.fori_loop(0, UNITS, unit_step, 0)

    def find_starts(u):
        span = span_of(u)
        token = span * BLOCK + lax.broadcasted_iota(jnp.int32, (BLOCK, HEAD_DIM), 0)
        start = jnp.zeros((BLOCK, HEAD_DIM), jnp.int32)
        end = jnp.int32(0)
        for j in range(NDOC):
            end = end + lengths[j]
            start = jnp.where(token >= end, end, start)
        starts[u] = start - (span - PAD) * BLOCK

    lane = lax.broadcasted_iota(jnp.int32, (BLOCK, 128), 1)
    row = lax.broadcasted_iota(jnp.int32, (BLOCK, 128), 0)

    def window_of(h, item, u):
        span = span_of(u)
        return jnp.concatenate([kv[h][item][places[span + n]] for n in range(WIN)], 0)

    def weigh(h, u):
        d, s = unit_of(u)
        q_rows = q_buf[h, lax.rem(NX - d, NX), pl.ds(pl.multiple_of(s * BLOCK, BLOCK), BLOCK), :]
        q = jnp.concatenate([q_rows[:, g * HEAD_DIM : (g + 1) * HEAD_DIM] for g in range(GROUP)], 0)
        keys_here = window_of(h, 0, u)
        start = starts[u]
        tops = [jnp.full((BLOCK, 128), -jnp.inf, jnp.float32)] * GROUP
        for first in range(0, WIN * BLOCK, 256):
            width = min(256, WIN * BLOCK - first)
            block = lax.dot_general(
                q, keys_here[first : first + width], (((1,), (1,)), ((), ())),
                preferred_element_type=jnp.float32,
            )
            for c in range(0, width, 128):
                allowed = lane + (first + c) >= start
                if first + c + 128 == WIN * BLOCK:
                    allowed = allowed & (lane - BLOCK <= row)
                for g in range(GROUP):
                    part = block[g * BLOCK : (g + 1) * BLOCK, c : c + 128]
                    part = jnp.where(allowed, part, -jnp.inf)
                    tops[g] = jnp.maximum(tops[g], part)
                    scores[(first + c) // 128, g * BLOCK : (g + 1) * BLOCK, :] = part
        for g in range(GROUP):
            rows = slice(g * BLOCK, (g + 1) * BLOCK)
            top = jnp.max(tops[g], axis=1, keepdims=True)
            total = jnp.zeros((BLOCK, 128), jnp.float32)
            for c in range(WIN // 2):
                part = jnp.exp2((scores[c, rows, :] - top) * SCALE)
                total = total + part
                weights[u, c, rows, :] = part.astype(jnp.bfloat16)
            total = jnp.sum(total, axis=1, keepdims=True)
            totals[u, rows, :] = jnp.broadcast_to(total, (BLOCK, HEAD_DIM))

    def o_rows(h, xx, s):
        return out.at[
            pl.ds(pl.multiple_of(s * BLOCK, BLOCK), BLOCK),
            pl.ds(pl.multiple_of(xx * QW + h * GW, GW), GW),
        ]

    def o_source(h, d, s):
        return o_buf.at[h, d, pl.ds(pl.multiple_of(s * BLOCK, BLOCK), BLOCK), :]

    def o_copy(h, d, s):
        sem = o_recv.at[h, d, s]
        return send(o_source(h, d, s), o_rows(h, x, s), o_send.at[h, d, s], sem, seq_of(at_x(d), z))

    def o_own(h, s):
        return pltpu.make_async_copy(o_source(h, 0, s), o_rows(h, x, s), o_recv.at[h, 0, s])

    def send_unit(h, u):
        d, s = unit_of(u)

        @pl.when(d > 0)
        def _():
            o_copy(h, d, s).start()

        @pl.when(d == 0)
        def _():
            o_own(h, s).start()

    def mix(h, u):
        d, s = unit_of(u)
        rounded = jnp.concatenate([weights[u, c] for c in range(WIN // 2)], 1)
        mixed = jnp.dot(rounded, window_of(h, 1, u), preferred_element_type=jnp.float32)
        mixed = (mixed / totals[u]).astype(jnp.bfloat16)
        for g in range(GROUP):
            o_buf[
                h, d, pl.ds(pl.multiple_of(s * BLOCK, BLOCK), BLOCK),
                g * HEAD_DIM : (g + 1) * HEAD_DIM,
            ] = mixed[g * BLOCK : (g + 1) * BLOCK]

        @pl.when(u > 0)
        def _():
            send_unit(h, u - 1)

    def q_wait(h):
        for d in range(NX):
            arrived(q_buf.at[h, d], q_recv.at[h, d])

    def forward(*step):
        return lambda: z_forward(*step)

    z_start(0, 0)
    run_units(find_starts)
    z_forward_both(0, 0, 2)
    z_forward_both(0, 0, 3)
    z_start(0, 1)
    z_forward(0, 0, 4, 0)
    z_forward_both(0, 1, 2)
    z_finish(0, 0)
    q_wait(0)
    run_units(
        functools.partial(weigh, 0),
        [(1, forward(0, 1, 3, 0)), (4, forward(0, 1, 3, 1)), (5, lambda: z_start(1, 0))],
    )
    z_forward(0, 1, 4, 0)
    z_forward_both(1, 0, 2)
    z_finish(0, 1)
    run_units(
        functools.partial(mix, 0),
        [(4, forward(1, 0, 3, 0)), (8, forward(1, 0, 3, 1)), (9, lambda: z_start(1, 1))],
    )
    send_unit(0, UNITS - 1)
    z_forward(1, 0, 4, 0)
    z_forward_both(1, 1, 2)
    z_finish(1, 0)
    q_wait(1)
    run_units(
        functools.partial(weigh, 1),
        [(4, forward(1, 1, 3, 0)), (8, forward(1, 1, 3, 1)), (12, forward(1, 1, 4, 0))],
    )
    z_finish(1, 1)
    run_units(functools.partial(mix, 1))
    send_unit(1, UNITS - 1)

    for h in range(KVH):
        for s in range(SPANS):
            o_own(h, s).wait()
            for d in range(1, NX):
                o_copy(h, d, s).wait_send()
                arrived(o_rows(h, at_x(NX - d), s), o_recv.at[h, d, s])
    for h in range(KVH):
        for d in range(1, NX):
            for item in range(2):
                x_copy(h, item, d).wait_send()
            q_copy(h, d).wait_send()
        for item in range(2):
            for way in range(2):
                for half in range(2):
                    for hop in range(1, 5 if half == way else 4):
                        z_copy(h, item, way, hop, half).wait_send()


def shards(queries, keys, values, lengths, span_order):
    spans = jnp.arange(NSPAN, dtype=jnp.int32)
    holder = spans // SPANS
    x = lax.axis_index("seq") // NZ
    slot = (x - holder // NZ + NX) % NX
    place = ((holder % NZ) * NX + slot) * SPANS + spans % SPANS
    padded = jnp.arange(-PAD, NSPAN, dtype=jnp.int32)
    places = jnp.sum(jnp.where(span_order[:, None] == padded[None, :], place[:, None], 0), axis=0)
    smem = pl.BlockSpec(memory_space=pltpu.SMEM)
    anywhere = pl.BlockSpec(memory_space=pl.ANY)
    dma = pltpu.SemaphoreType.DMA
    return pl.pallas_call(
        body,
        out_shape=jax.ShapeDtypeStruct((ROWS, HEADS * HEAD_DIM), jnp.bfloat16),
        in_specs=[smem, smem, smem, anywhere, anywhere, anywhere],
        out_specs=anywhere,
        scratch_shapes=[
            *[pltpu.VMEM((NSPAN, BLOCK, HEAD_DIM), jnp.bfloat16)] * (2 * KVH),
            pltpu.VMEM((KVH, NX, ROWS, GW), jnp.bfloat16),
            pltpu.VMEM((KVH, NX, ROWS, GW), jnp.bfloat16),
            pltpu.VMEM((UNITS, BLOCK, HEAD_DIM), jnp.int32),
            pltpu.VMEM((WIN // 2, GROUP * BLOCK, 128), jnp.float32),
            pltpu.VMEM((UNITS, WIN // 2, GROUP * BLOCK, 128), jnp.bfloat16),
            pltpu.VMEM((UNITS, GROUP * BLOCK, HEAD_DIM), jnp.float32),
            dma((KVH, 2, NX)),
            dma((KVH, 2, NX)),
            dma((KVH, NX)),
            dma((KVH, NX)),
            dma((KVH, 2, 2, 4, 2)),
            dma((KVH, 2, 2, 4, 2)),
            dma((KVH, NX, SPANS)),
            dma((KVH, NX, SPANS)),
        ],
        compiler_params=pltpu.CompilerParams(collective_id=0, has_side_effects=True),
        name="span_attention",
    )(
        lengths, span_order, places.astype(jnp.int32), queries,
        keys.reshape(SPANS, BLOCK, KV_HEADS * HEAD_DIM),
        values.reshape(SPANS, BLOCK, KV_HEADS * HEAD_DIM),
    )


def solution(mesh):
    placed = (
        P(("dp", "seq"), None),
        P(("dp", "seq"), None),
        P(("dp", "seq"), None),
        P("dp"),
        P("dp"),
    )
    return jax.shard_map(
        shards, mesh=mesh, in_specs=placed, out_specs=P(("dp", "seq"), None), check_vma=False
    )
```

```python
import functools
import math

import jax
import jax.numpy as jnp
from jax import lax
from jax.experimental import pallas as pl
from jax.experimental.pallas import tpu as pltpu
from jax.sharding import PartitionSpec as P

HEADS = 32
KV_HEADS = 8
HEAD_DIM = 128
BLOCK = 64
NX = 4
NZ = 8
ROWS = 256
SPANS = ROWS // BLOCK
GROUP = HEADS // KV_HEADS
KVH = KV_HEADS // NX
QW = HEADS * HEAD_DIM // NX
GW = GROUP * HEAD_DIM
TOKENS = NX * NZ * ROWS
NSPAN = TOKENS // BLOCK
PAD = 17
WIN = 18
UNITS = NX * SPANS
HALF = UNITS // 2
NDOC = 32
SCALE = HEAD_DIM**-0.5 * math.log2(math.e)


def body(
    lengths, order, places, queries, keys, values, out,
    k_first, v_first, k_second, v_second, q_buf, o_buf, starts, scores, weights, totals,
    x_send, x_recv, q_send, q_recv, own_send, own_recv, z_send, z_recv, o_send, o_recv,
):
    me = lax.axis_index("seq")
    x = me // NZ
    z = lax.rem(me, NZ)
    kv = ((k_first, v_first), (k_second, v_second))

    def at_x(offset):
        return lax.rem(x + offset, NX)

    def at_z(offset):
        return lax.rem(z + offset + NZ, NZ)

    def seq_of(xx, zz):
        return {"seq": xx * NZ + zz}

    def send(src_ref, dst_ref, send_sem, recv_sem, target):
        return pltpu.make_async_remote_copy(
            src_ref=src_ref,
            dst_ref=dst_ref,
            send_sem=send_sem,
            recv_sem=recv_sem,
            device_id=target,
            device_id_type=pl.DeviceIdType.MESH,
        )

    def arrived(ref, sem):
        pltpu.make_async_copy(ref, ref, sem).wait()

    barrier = pltpu.get_barrier_semaphore()
    partners = [seq_of(at_x(d), z) for d in range(1, NX)]
    partners += [seq_of(x, at_z(1)), seq_of(x, at_z(-1))]
    for partner in partners:
        pl.semaphore_signal(barrier, inc=1, device_id=partner, device_id_type=pl.DeviceIdType.MESH)
    pl.semaphore_wait(barrier, len(partners))

    def kv_rows(h, item, zz, d):
        return kv[h][item].at[pl.ds(zz * UNITS + d * SPANS, SPANS)]

    def kv_source(h, item, d):
        first = pl.multiple_of(at_x(d) * (KVH * HEAD_DIM) + h * HEAD_DIM, HEAD_DIM)
        return (keys, values)[item].at[:, :, pl.ds(first, HEAD_DIM)]

    def x_copy(h, item, d):
        source, target, sem = kv_source(h, item, d), kv_rows(h, item, z, d), x_recv.at[h, item, d]
        if d == 0:
            return pltpu.make_async_copy(source, target, sem)
        return send(source, target, x_send.at[h, item, d], sem, seq_of(at_x(d), z))

    def q_copy(h, d):
        source = queries.at[:, pl.ds(pl.multiple_of(at_x(d) * QW + h * GW, GW), GW)]
        target, sem = q_buf.at[h, d], q_recv.at[h, d]
        if d == 0:
            return pltpu.make_async_copy(source, target, sem)
        return send(source, target, q_send.at[h, d], sem, seq_of(at_x(d), z))

    for h in range(KVH):
        for item in range(2):
            for d in range(NX):
                x_copy(h, item, d).start()
        for d in range(NX):
            q_copy(h, d).start()

    def piece(h, item, half, zz):
        return kv[h][item].at[pl.ds(zz * UNITS + half * HALF, HALF)]

    def z_copy(h, item, way, hop, half):
        turn = 1 - 2 * way
        ref = piece(h, item, half, at_z(-turn * (hop - 1)))
        sems = (h, item, way, hop - 2, half)
        return send(ref, ref, z_send.at[sems], z_recv.at[sems], seq_of(x, at_z(turn)))

    def z_own(h, item, way, d):
        ref, sems = kv_rows(h, item, z, d), (h, item, way, d)
        return send(ref, ref, own_send.at[sems], own_recv.at[sems], seq_of(x, at_z(1 - 2 * way)))

    def z_arrived(h, item, way, hop, half):
        source = at_z((2 * way - 1) * hop)
        if hop > 1:
            arrived(piece(h, item, half, source), z_recv.at[h, item, way, hop - 2, half])
        else:
            for d in (2 * half, 2 * half + 1):
                arrived(kv_rows(h, item, source, d), own_recv.at[h, item, way, d])

    def z_start(h, item):
        for d in range(NX):
            arrived(kv_rows(h, item, z, d), x_recv.at[h, item, d])
            for way in range(2):
                z_own(h, item, way, d).start()

    def z_forward(h, item, hop, half):
        for way in range(2):
            part = half if hop < 4 else way
            z_arrived(h, item, way, hop - 1, part)
            z_copy(h, item, way, hop, part).start()

    def z_forward_both(h, item, hop):
        for half in range(2):
            z_forward(h, item, hop, half)

    def z_finish(h, item):
        for way in range(2):
            z_arrived(h, item, way, 3, 1 - way)
        for way in range(2):
            z_arrived(h, item, way, 4, way)

    def unit_of(u):
        d = lax.rem(lax.rem(u, NX) + 1, NX)
        return d, u // NX

    def span_of(u):
        d, s = unit_of(u)
        return order[(at_x(d) * NZ + z) * SPANS + s]

    def run_units(step, events=()):
        def unit_step(u, carry):
            for when, event in events:
                pl.when(u == when)(event)
            step(u)
            return carry

        lax.fori_loop(0, UNITS, unit_step, 0)

    def find_starts(u):
        span = span_of(u)
        token = span * BLOCK + lax.broadcasted_iota(jnp.int32, (BLOCK, HEAD_DIM), 0)
        start = jnp.zeros((BLOCK, HEAD_DIM), jnp.int32)
        end = jnp.int32(0)
        for j in range(NDOC):
            end = end + lengths[j]
            start = jnp.where(token >= end, end, start)
        starts[u] = start - (span - PAD) * BLOCK

    lane = lax.broadcasted_iota(jnp.int32, (BLOCK, 128), 1)
    row = lax.broadcasted_iota(jnp.int32, (BLOCK, 128), 0)

    def window_of(h, item, u):
        span = span_of(u)
        return jnp.concatenate([kv[h][item][places[span + n]] for n in range(WIN)], 0)

    def weigh(h, u):
        d, s = unit_of(u)
        q_rows = q_buf[h, lax.rem(NX - d, NX), pl.ds(pl.multiple_of(s * BLOCK, BLOCK), BLOCK), :]
        q = jnp.concatenate([q_rows[:, g * HEAD_DIM : (g + 1) * HEAD_DIM] for g in range(GROUP)], 0)
        keys_here = window_of(h, 0, u)
        start = starts[u]
        tops = [jnp.full((BLOCK, 128), -jnp.inf, jnp.float32)] * GROUP
        for first in range(0, WIN * BLOCK, 256):
            width = min(256, WIN * BLOCK - first)
            block = lax.dot_general(
                q, keys_here[first : first + width], (((1,), (1,)), ((), ())),
                preferred_element_type=jnp.float32,
            )
            for c in range(0, width, 128):
                allowed = lane + (first + c) >= start
                if first + c + 128 == WIN * BLOCK:
                    allowed = allowed & (lane - BLOCK <= row)
                for g in range(GROUP):
                    part = block[g * BLOCK : (g + 1) * BLOCK, c : c + 128]
                    part = jnp.where(allowed, part, -jnp.inf)
                    tops[g] = jnp.maximum(tops[g], part)
                    scores[(first + c) // 128, g * BLOCK : (g + 1) * BLOCK, :] = part
        for g in range(GROUP):
            rows = slice(g * BLOCK, (g + 1) * BLOCK)
            top = jnp.max(tops[g], axis=1, keepdims=True)
            total = jnp.zeros((BLOCK, 128), jnp.float32)
            for c in range(WIN // 2):
                part = jnp.exp2((scores[c, rows, :] - top) * SCALE)
                total = total + part
                weights[u, c, rows, :] = part.astype(jnp.bfloat16)
            total = jnp.sum(total, axis=1, keepdims=True)
            totals[u, rows, :] = jnp.broadcast_to(total, (BLOCK, HEAD_DIM))

    def o_rows(h, xx, s):
        return out.at[
            pl.ds(pl.multiple_of(s * BLOCK, BLOCK), BLOCK),
            pl.ds(pl.multiple_of(xx * QW + h * GW, GW), GW),
        ]

    def o_source(h, d, s):
        return o_buf.at[h, d, pl.ds(pl.multiple_of(s * BLOCK, BLOCK), BLOCK), :]

    def o_copy(h, d, s):
        sem = o_recv.at[h, d, s]
        return send(o_source(h, d, s), o_rows(h, x, s), o_send.at[h, d, s], sem, seq_of(at_x(d), z))

    def o_own(h, s):
        return pltpu.make_async_copy(o_source(h, 0, s), o_rows(h, x, s), o_recv.at[h, 0, s])

    def send_unit(h, u):
        d, s = unit_of(u)

        @pl.when(d > 0)
        def _():
            o_copy(h, d, s).start()

        @pl.when(d == 0)
        def _():
            o_own(h, s).start()

    def mix(h, u):
        d, s = unit_of(u)
        rounded = jnp.concatenate([weights[u, c] for c in range(WIN // 2)], 1)
        mixed = jnp.dot(rounded, window_of(h, 1, u), preferred_element_type=jnp.float32)
        mixed = (mixed / totals[u]).astype(jnp.bfloat16)
        for g in range(GROUP):
            o_buf[
                h, d, pl.ds(pl.multiple_of(s * BLOCK, BLOCK), BLOCK),
                g * HEAD_DIM : (g + 1) * HEAD_DIM,
            ] = mixed[g * BLOCK : (g + 1) * BLOCK]

        @pl.when(u > 0)
        def _():
            send_unit(h, u - 1)

    def q_wait(h):
        for d in range(NX):
            arrived(q_buf.at[h, d], q_recv.at[h, d])

    def forward(*step):
        return lambda: z_forward(*step)

    z_start(0, 0)
    run_units(find_starts)
    z_forward_both(0, 0, 2)
    z_forward_both(0, 0, 3)
    z_start(0, 1)
    z_forward(0, 0, 4, 0)
    z_forward_both(0, 1, 2)
    z_finish(0, 0)
    q_wait(0)
    run_units(
        functools.partial(weigh, 0),
        [(1, forward(0, 1, 3, 0)), (4, forward(0, 1, 3, 1)), (5, lambda: z_start(1, 0))],
    )
    z_forward(0, 1, 4, 0)
    z_forward_both(1, 0, 2)
    z_finish(0, 1)
    run_units(
        functools.partial(mix, 0),
        [(4, forward(1, 0, 3, 0)), (8, forward(1, 0, 3, 1)), (9, lambda: z_start(1, 1))],
    )
    send_unit(0, UNITS - 1)
    z_forward(1, 0, 4, 0)
    z_forward_both(1, 1, 2)
    z_finish(1, 0)
    q_wait(1)
    run_units(
        functools.partial(weigh, 1),
        [(4, forward(1, 1, 3, 0)), (8, forward(1, 1, 3, 1)), (12, forward(1, 1, 4, 0))],
    )
    z_finish(1, 1)
    run_units(functools.partial(mix, 1))
    send_unit(1, UNITS - 1)

    for h in range(KVH):
        for s in range(SPANS):
            o_own(h, s).wait()
            for d in range(1, NX):
                o_copy(h, d, s).wait_send()
                arrived(o_rows(h, at_x(NX - d), s), o_recv.at[h, d, s])
    for h in range(KVH):
        for d in range(1, NX):
            for item in range(2):
                x_copy(h, item, d).wait_send()
            q_copy(h, d).wait_send()
        for item in range(2):
            for way in range(2):
                for d in range(NX):
                    z_own(h, item, way, d).wait_send()
                for half in range(2):
                    for hop in range(2, 5 if half == way else 4):
                        z_copy(h, item, way, hop, half).wait_send()


def shards(queries, keys, values, lengths, span_order):
    spans = jnp.arange(NSPAN, dtype=jnp.int32)
    holder = spans // SPANS
    x = lax.axis_index("seq") // NZ
    slot = (x - holder // NZ + NX) % NX
    place = ((holder % NZ) * NX + slot) * SPANS + spans % SPANS
    padded = jnp.arange(-PAD, NSPAN, dtype=jnp.int32)
    places = jnp.sum(jnp.where(span_order[:, None] == padded[None, :], place[:, None], 0), axis=0)
    smem = pl.BlockSpec(memory_space=pltpu.SMEM)
    anywhere = pl.BlockSpec(memory_space=pl.ANY)
    dma = pltpu.SemaphoreType.DMA
    return pl.pallas_call(
        body,
        out_shape=pltpu.VMEM((ROWS, HEADS * HEAD_DIM), jnp.bfloat16),
        in_specs=[smem, smem, smem, anywhere, anywhere, anywhere],
        out_specs=pl.BlockSpec(memory_space=pltpu.VMEM),
        scratch_shapes=[
            *[pltpu.VMEM((NSPAN, BLOCK, HEAD_DIM), jnp.bfloat16)] * (2 * KVH),
            pltpu.VMEM((KVH, NX, ROWS, GW), jnp.bfloat16),
            pltpu.VMEM((KVH, NX, ROWS, GW), jnp.bfloat16),
            pltpu.VMEM((UNITS, BLOCK, HEAD_DIM), jnp.int32),
            pltpu.VMEM((WIN // 2, GROUP * BLOCK, 128), jnp.float32),
            pltpu.VMEM((UNITS, WIN // 2, GROUP * BLOCK, 128), jnp.bfloat16),
            pltpu.VMEM((UNITS, GROUP * BLOCK, HEAD_DIM), jnp.float32),
            dma((KVH, 2, NX)),
            dma((KVH, 2, NX)),
            dma((KVH, NX)),
            dma((KVH, NX)),
            dma((KVH, 2, 2, NX)),
            dma((KVH, 2, 2, NX)),
            dma((KVH, 2, 2, 3, 2)),
            dma((KVH, 2, 2, 3, 2)),
            dma((KVH, NX, SPANS)),
            dma((KVH, NX, SPANS)),
        ],
        compiler_params=pltpu.CompilerParams(
            collective_id=0, has_side_effects=True, vmem_limit_bytes=58 * 2**20
        ),
        name="span_attention",
    )(
        lengths, span_order, places.astype(jnp.int32), queries,
        keys.reshape(SPANS, BLOCK, KV_HEADS * HEAD_DIM),
        values.reshape(SPANS, BLOCK, KV_HEADS * HEAD_DIM),
    )


def solution(mesh):
    placed = (
        P(("dp", "seq"), None),
        P(("dp", "seq"), None),
        P(("dp", "seq"), None),
        P("dp"),
        P("dp"),
    )
    return jax.shard_map(
        shards, mesh=mesh, in_specs=placed, out_specs=P(("dp", "seq"), None), check_vma=False
    )
```

```python
import functools
import math

import jax
import jax.numpy as jnp
from jax import lax
from jax.experimental import pallas as pl
from jax.experimental.pallas import tpu as pltpu
from jax.sharding import PartitionSpec as P

HEADS = 32
KV_HEADS = 8
HEAD_DIM = 128
BLOCK = 64
NX = 4
NZ = 8
ROWS = 256
SPANS = ROWS // BLOCK
GROUP = HEADS // KV_HEADS
KVH = KV_HEADS // NX
QW = HEADS * HEAD_DIM // NX
GW = GROUP * HEAD_DIM
TOKENS = NX * NZ * ROWS
NSPAN = TOKENS // BLOCK
PAD = 17
WIN = 18
UNITS = NX * SPANS
HALF = UNITS // 2
NDOC = 32
SCALE = HEAD_DIM**-0.5 * math.log2(math.e)


def body(
    lengths, order, order_row, queries, keys, values, out,
    k_first, v_first, k_second, v_second, q_buf, o_buf, places, starts, scores, weights, totals,
    x_send, x_recv, q_send, q_recv, own_send, own_recv, z_send, z_recv, o_send, o_recv,
):
    me = lax.axis_index("seq")
    x = me // NZ
    z = lax.rem(me, NZ)
    kv = ((k_first, v_first), (k_second, v_second))

    def at_x(offset):
        return lax.rem(x + offset, NX)

    def at_z(offset):
        return lax.rem(z + offset + NZ, NZ)

    def seq_of(xx, zz):
        return {"seq": xx * NZ + zz}

    def send(src_ref, dst_ref, send_sem, recv_sem, target):
        return pltpu.make_async_remote_copy(
            src_ref=src_ref,
            dst_ref=dst_ref,
            send_sem=send_sem,
            recv_sem=recv_sem,
            device_id=target,
            device_id_type=pl.DeviceIdType.MESH,
        )

    def arrived(ref, sem):
        pltpu.make_async_copy(ref, ref, sem).wait()

    barrier = pltpu.get_barrier_semaphore()
    partners = [seq_of(at_x(d), z) for d in range(1, NX)]
    partners += [seq_of(x, at_z(1)), seq_of(x, at_z(-1))]
    for partner in partners:
        pl.semaphore_signal(barrier, inc=1, device_id=partner, device_id_type=pl.DeviceIdType.MESH)
    pl.semaphore_wait(barrier, len(partners))

    def kv_rows(h, item, zz, d):
        return kv[h][item].at[pl.ds(zz * UNITS + d * SPANS, SPANS)]

    def kv_source(h, item, d):
        first = pl.multiple_of(at_x(d) * (KVH * HEAD_DIM) + h * HEAD_DIM, HEAD_DIM)
        return (keys, values)[item].at[:, :, pl.ds(first, HEAD_DIM)]

    def x_copy(h, item, d):
        source, target, sem = kv_source(h, item, d), kv_rows(h, item, z, d), x_recv.at[h, item, d]
        if d == 0:
            return pltpu.make_async_copy(source, target, sem)
        return send(source, target, x_send.at[h, item, d], sem, seq_of(at_x(d), z))

    def q_copy(h, d):
        source = queries.at[:, pl.ds(pl.multiple_of(at_x(d) * QW + h * GW, GW), GW)]
        target, sem = q_buf.at[h, d], q_recv.at[h, d]
        if d == 0:
            return pltpu.make_async_copy(source, target, sem)
        return send(source, target, q_send.at[h, d], sem, seq_of(at_x(d), z))

    for h in range(KVH):
        for item in range(2):
            for d in range(NX):
                x_copy(h, item, d).start()
        for d in range(NX):
            q_copy(h, d).start()

    def piece(h, item, half, zz):
        return kv[h][item].at[pl.ds(zz * UNITS + half * HALF, HALF)]

    def z_copy(h, item, way, hop, half):
        turn = 1 - 2 * way
        ref = piece(h, item, half, at_z(-turn * (hop - 1)))
        sems = (h, item, way, hop - 2, half)
        return send(ref, ref, z_send.at[sems], z_recv.at[sems], seq_of(x, at_z(turn)))

    def z_own(h, item, way, d):
        ref, sems = kv_rows(h, item, z, d), (h, item, way, d)
        return send(ref, ref, own_send.at[sems], own_recv.at[sems], seq_of(x, at_z(1 - 2 * way)))

    def z_arrived(h, item, way, hop, half):
        source = at_z((2 * way - 1) * hop)
        if hop > 1:
            arrived(piece(h, item, half, source), z_recv.at[h, item, way, hop - 2, half])
        else:
            for d in (2 * half, 2 * half + 1):
                arrived(kv_rows(h, item, source, d), own_recv.at[h, item, way, d])

    def z_start(h, item):
        for d in range(NX):
            arrived(kv_rows(h, item, z, d), x_recv.at[h, item, d])
            for way in range(2):
                z_own(h, item, way, d).start()

    def z_forward(h, item, hop, half):
        for way in range(2):
            part = half if hop < 4 else way
            z_arrived(h, item, way, hop - 1, part)
            z_copy(h, item, way, hop, part).start()

    def z_forward_both(h, item, hop):
        for half in range(2):
            z_forward(h, item, hop, half)

    def z_finish(h, item):
        for way in range(2):
            z_arrived(h, item, way, 3, 1 - way)
        for way in range(2):
            z_arrived(h, item, way, 4, way)

    def unit_of(u):
        turn = lax.rem(u, NX)
        return lax.rem(1 + 2 * turn + turn // 2, NX), u // NX

    def span_of(u):
        d, s = unit_of(u)
        return order[(at_x(d) * NZ + z) * SPANS + s]

    def find_places(part):
        span = lax.broadcasted_iota(jnp.int32, (1, NSPAN), 1)
        slot = (x - span // (SPANS * NZ) + NX) & (NX - 1)
        place = ((span // SPANS) & (NZ - 1)) * UNITS + slot * SPANS + (span & (SPANS - 1))
        loader = order_row[...]

        def some(i, carry):
            for n in range(8):
                t = (4 * part + i) * 8 + n
                places[PAD + t] = jnp.max(jnp.where(loader == t, place, 0))
            return carry

        lax.fori_loop(0, 4, some, 0)

    def run_units(step, events=()):
        def unit_step(u, carry):
            for when, event in events:
                pl.when(u == when)(event)
            step(u)
            return carry

        lax.fori_loop(0, UNITS, unit_step, 0)

    def find_starts(u):
        span = span_of(u)
        token = span * BLOCK + lax.broadcasted_iota(jnp.int32, (BLOCK, HEAD_DIM), 0)
        start = jnp.zeros((BLOCK, HEAD_DIM), jnp.int32)
        end = jnp.int32(0)
        for j in range(NDOC):
            end = end + lengths[j]
            start = jnp.where(token >= end, end, start)
        starts[u] = start - (span - PAD) * BLOCK

    lane = lax.broadcasted_iota(jnp.int32, (BLOCK, 128), 1)
    row = lax.broadcasted_iota(jnp.int32, (BLOCK, 128), 0)

    def window_of(h, item, u):
        span = span_of(u)
        return jnp.concatenate([kv[h][item][places[span + n]] for n in range(WIN)], 0)

    def weigh(h, u):
        d, s = unit_of(u)
        q_rows = q_buf[h, lax.rem(NX - d, NX), pl.ds(pl.multiple_of(s * BLOCK, BLOCK), BLOCK), :]
        q = jnp.concatenate([q_rows[:, g * HEAD_DIM : (g + 1) * HEAD_DIM] for g in range(GROUP)], 0)
        keys_here = window_of(h, 0, u)
        start = starts[u]
        tops = [jnp.full((BLOCK, 128), -jnp.inf, jnp.float32)] * GROUP
        for first in range(0, WIN * BLOCK, 256):
            width = min(256, WIN * BLOCK - first)
            block = lax.dot_general(
                q, keys_here[first : first + width], (((1,), (1,)), ((), ())),
                preferred_element_type=jnp.float32,
            )
            for c in range(0, width, 128):
                allowed = lane + (first + c) >= start
                if first + c + 128 == WIN * BLOCK:
                    allowed = allowed & (lane - BLOCK <= row)
                for g in range(GROUP):
                    part = block[g * BLOCK : (g + 1) * BLOCK, c : c + 128]
                    part = jnp.where(allowed, part, -jnp.inf)
                    tops[g] = jnp.maximum(tops[g], part)
                    scores[(first + c) // 128, g * BLOCK : (g + 1) * BLOCK, :] = part
        for g in range(GROUP):
            rows = slice(g * BLOCK, (g + 1) * BLOCK)
            top = jnp.max(tops[g], axis=1, keepdims=True)
            total = jnp.zeros((BLOCK, 128), jnp.float32)
            for c in range(WIN // 2):
                part = jnp.exp2((scores[c, rows, :] - top) * SCALE)
                total = total + part
                weights[u, c, rows, :] = part.astype(jnp.bfloat16)
            total = jnp.sum(total, axis=1, keepdims=True)
            totals[u, rows, :] = jnp.broadcast_to(total, (BLOCK, HEAD_DIM))

    def o_rows(h, xx, s):
        return out.at[
            pl.ds(pl.multiple_of(s * BLOCK, BLOCK), BLOCK),
            pl.ds(pl.multiple_of(xx * QW + h * GW, GW), GW),
        ]

    def o_source(h, d, s):
        return o_buf.at[h, d, pl.ds(pl.multiple_of(s * BLOCK, BLOCK), BLOCK), :]

    def o_copy(h, d, s):
        sem = o_recv.at[h, d, s]
        return send(o_source(h, d, s), o_rows(h, x, s), o_send.at[h, d, s], sem, seq_of(at_x(d), z))

    def o_own(h, s):
        return pltpu.make_async_copy(o_source(h, 0, s), o_rows(h, x, s), o_recv.at[h, 0, s])

    def send_unit(h, u):
        d, s = unit_of(u)

        @pl.when(d > 0)
        def _():
            o_copy(h, d, s).start()

        @pl.when(d == 0)
        def _():
            o_own(h, s).start()

    def mix(h, u):
        d, s = unit_of(u)
        rounded = jnp.concatenate([weights[u, c] for c in range(WIN // 2)], 1)
        mixed = jnp.dot(rounded, window_of(h, 1, u), preferred_element_type=jnp.float32)
        mixed = (mixed / totals[u]).astype(jnp.bfloat16)
        for g in range(GROUP):
            o_buf[
                h, d, pl.ds(pl.multiple_of(s * BLOCK, BLOCK), BLOCK),
                g * HEAD_DIM : (g + 1) * HEAD_DIM,
            ] = mixed[g * BLOCK : (g + 1) * BLOCK]

        @pl.when(u > 0)
        def _():
            send_unit(h, u - 1)

    def q_wait(h):
        for d in range(NX):
            arrived(q_buf.at[h, d], q_recv.at[h, d])

    def forward(*step):
        return lambda: z_forward(*step)

    z_start(0, 0)
    for n in range(PAD):
        places[n] = 0
    find_places(0)
    z_forward_both(0, 0, 2)
    find_places(1)
    z_forward_both(0, 0, 3)
    z_start(0, 1)
    find_places(2)
    z_forward(0, 0, 4, 0)
    run_units(find_starts)
    z_forward_both(0, 1, 2)
    find_places(3)
    z_finish(0, 0)
    q_wait(0)
    run_units(
        functools.partial(weigh, 0),
        [(1, forward(0, 1, 3, 0)), (4, forward(0, 1, 3, 1)), (5, lambda: z_start(1, 0))],
    )
    z_forward(0, 1, 4, 0)
    z_forward_both(1, 0, 2)
    z_finish(0, 1)
    run_units(
        functools.partial(mix, 0),
        [(4, forward(1, 0, 3, 0)), (8, forward(1, 0, 3, 1)), (9, lambda: z_start(1, 1))],
    )
    send_unit(0, UNITS - 1)
    z_forward(1, 0, 4, 0)
    z_forward_both(1, 1, 2)
    z_finish(1, 0)
    q_wait(1)
    run_units(
        functools.partial(weigh, 1),
        [(4, forward(1, 1, 3, 0)), (8, forward(1, 1, 3, 1)), (12, forward(1, 1, 4, 0))],
    )
    z_finish(1, 1)
    run_units(functools.partial(mix, 1))
    send_unit(1, UNITS - 1)

    for h in range(KVH):
        for s in range(SPANS):
            o_own(h, s).wait()
            for d in range(1, NX):
                o_copy(h, d, s).wait_send()
                arrived(o_rows(h, at_x(NX - d), s), o_recv.at[h, d, s])
    for h in range(KVH):
        for d in range(1, NX):
            for item in range(2):
                x_copy(h, item, d).wait_send()
            q_copy(h, d).wait_send()
        for item in range(2):
            for way in range(2):
                for d in range(NX):
                    z_own(h, item, way, d).wait_send()
                for half in range(2):
                    for hop in range(2, 5 if half == way else 4):
                        z_copy(h, item, way, hop, half).wait_send()


def shards(queries, keys, values, lengths, span_order):
    smem = pl.BlockSpec(memory_space=pltpu.SMEM)
    vmem = pl.BlockSpec(memory_space=pltpu.VMEM)
    anywhere = pl.BlockSpec(memory_space=pl.ANY)
    dma = pltpu.SemaphoreType.DMA
    return pl.pallas_call(
        body,
        out_shape=pltpu.VMEM((ROWS, HEADS * HEAD_DIM), jnp.bfloat16),
        in_specs=[smem, smem, vmem, anywhere, anywhere, anywhere],
        out_specs=vmem,
        scratch_shapes=[
            *[pltpu.VMEM((NSPAN, BLOCK, HEAD_DIM), jnp.bfloat16)] * (2 * KVH),
            pltpu.VMEM((KVH, NX, ROWS, GW), jnp.bfloat16),
            pltpu.VMEM((KVH, NX, ROWS, GW), jnp.bfloat16),
            pltpu.SMEM((PAD + NSPAN,), jnp.int32),
            pltpu.VMEM((UNITS, BLOCK, HEAD_DIM), jnp.int32),
            pltpu.VMEM((WIN // 2, GROUP * BLOCK, 128), jnp.float32),
            pltpu.VMEM((UNITS, WIN // 2, GROUP * BLOCK, 128), jnp.bfloat16),
            pltpu.VMEM((UNITS, GROUP * BLOCK, HEAD_DIM), jnp.float32),
            dma((KVH, 2, NX)),
            dma((KVH, 2, NX)),
            dma((KVH, NX)),
            dma((KVH, NX)),
            dma((KVH, 2, 2, NX)),
            dma((KVH, 2, 2, NX)),
            dma((KVH, 2, 2, 3, 2)),
            dma((KVH, 2, 2, 3, 2)),
            dma((KVH, NX, SPANS)),
            dma((KVH, NX, SPANS)),
        ],
        compiler_params=pltpu.CompilerParams(
            collective_id=0, has_side_effects=True, vmem_limit_bytes=58 * 2**20
        ),
        name="span_attention",
    )(
        lengths, span_order, span_order.reshape(1, NSPAN), queries,
        keys.reshape(SPANS, BLOCK, KV_HEADS * HEAD_DIM),
        values.reshape(SPANS, BLOCK, KV_HEADS * HEAD_DIM),
    )


def solution(mesh):
    placed = (
        P(("dp", "seq"), None),
        P(("dp", "seq"), None),
        P(("dp", "seq"), None),
        P("dp"),
        P("dp"),
    )
    return jax.shard_map(
        shards, mesh=mesh, in_specs=placed, out_specs=P(("dp", "seq"), None), check_vma=False
    )
```

```python
import functools
import math

import jax
import jax.numpy as jnp
from jax import lax
from jax.experimental import pallas as pl
from jax.experimental.pallas import tpu as pltpu
from jax.sharding import PartitionSpec as P

HEADS = 32
KV_HEADS = 8
HEAD_DIM = 128
BLOCK = 64
NX = 4
NZ = 8
ROWS = 256
SPANS = ROWS // BLOCK
GROUP = HEADS // KV_HEADS
KVH = KV_HEADS // NX
QW = HEADS * HEAD_DIM // NX
GW = GROUP * HEAD_DIM
TOKENS = NX * NZ * ROWS
NSPAN = TOKENS // BLOCK
PAD = 17
WIN = 18
UNITS = NX * SPANS
HALF = UNITS // 2
NDOC = 32
SCALE = HEAD_DIM**-0.5 * math.log2(math.e)


def body(
    lengths, order, order_row, queries, keys, values, out,
    k_first, v_first, k_second, v_second, q_buf, o_buf, places, starts, scores, weights, totals,
    x_send, x_recv, q_send, q_recv, own_send, own_recv, z_send, z_recv, o_send, o_recv,
):
    me = lax.axis_index("seq")
    x = me // NZ
    z = lax.rem(me, NZ)
    kv = ((k_first, v_first), (k_second, v_second))

    def at_x(offset):
        return lax.rem(x + offset, NX)

    def at_z(offset):
        return lax.rem(z + offset + NZ, NZ)

    def seq_of(xx, zz):
        return {"seq": xx * NZ + zz}

    def send(src_ref, dst_ref, send_sem, recv_sem, target):
        return pltpu.make_async_remote_copy(
            src_ref=src_ref,
            dst_ref=dst_ref,
            send_sem=send_sem,
            recv_sem=recv_sem,
            device_id=target,
            device_id_type=pl.DeviceIdType.MESH,
        )

    def arrived(ref, sem):
        pltpu.make_async_copy(ref, ref, sem).wait()

    barrier = pltpu.get_barrier_semaphore()
    partners = [seq_of(at_x(d), z) for d in range(1, NX)]
    partners += [seq_of(x, at_z(1)), seq_of(x, at_z(-1))]
    for partner in partners:
        pl.semaphore_signal(barrier, inc=1, device_id=partner, device_id_type=pl.DeviceIdType.MESH)
    pl.semaphore_wait(barrier, len(partners))

    def kv_rows(h, item, zz, d):
        return kv[h][item].at[pl.ds(zz * UNITS + d * SPANS, SPANS)]

    def kv_source(h, item, d):
        first = pl.multiple_of(at_x(d) * (KVH * HEAD_DIM) + h * HEAD_DIM, HEAD_DIM)
        return (keys, values)[item].at[:, :, pl.ds(first, HEAD_DIM)]

    def x_copy(h, item, d):
        source, target, sem = kv_source(h, item, d), kv_rows(h, item, z, d), x_recv.at[h, item, d]
        if d == 0:
            return pltpu.make_async_copy(source, target, sem)
        return send(source, target, x_send.at[h, item, d], sem, seq_of(at_x(d), z))

    def q_copy(h, d):
        source = queries.at[:, pl.ds(pl.multiple_of(at_x(d) * QW + h * GW, GW), GW)]
        target, sem = q_buf.at[h, d], q_recv.at[h, d]
        if d == 0:
            return pltpu.make_async_copy(source, target, sem)
        return send(source, target, q_send.at[h, d], sem, seq_of(at_x(d), z))

    for h in range(KVH):
        for item in range(2):
            for d in range(NX):
                x_copy(h, item, d).start()
        for d in range(NX):
            q_copy(h, d).start()

    def piece(h, item, half, zz):
        return kv[h][item].at[pl.ds(zz * UNITS + half * HALF, HALF)]

    def z_copy(h, item, way, hop, half):
        turn = 1 - 2 * way
        ref = piece(h, item, half, at_z(-turn * (hop - 1)))
        sems = (h, item, way, hop - 2, half)
        return send(ref, ref, z_send.at[sems], z_recv.at[sems], seq_of(x, at_z(turn)))

    def z_own(h, item, way, d):
        ref, sems = kv_rows(h, item, z, d), (h, item, way, d)
        return send(ref, ref, own_send.at[sems], own_recv.at[sems], seq_of(x, at_z(1 - 2 * way)))

    def z_arrived(h, item, way, hop, half):
        source = at_z((2 * way - 1) * hop)
        if hop > 1:
            arrived(piece(h, item, half, source), z_recv.at[h, item, way, hop - 2, half])
        else:
            for d in (2 * half, 2 * half + 1):
                arrived(kv_rows(h, item, source, d), own_recv.at[h, item, way, d])

    def z_start(h, item):
        for d in range(NX):
            arrived(kv_rows(h, item, z, d), x_recv.at[h, item, d])
            for way in range(2):
                z_own(h, item, way, d).start()

    def z_forward(h, item, hop, half):
        for way in range(2):
            lead = way if (h, item) == (1, 1) else 0
            part = way if hop == 4 else (half + lead) % 2
            z_arrived(h, item, way, hop - 1, part)
            z_copy(h, item, way, hop, part).start()

    def z_forward_both(h, item, hop):
        for half in range(2):
            z_forward(h, item, hop, half)

    def z_finish(h, item):
        for way in range(2):
            z_arrived(h, item, way, 3, 1 - way)
        for way in range(2):
            z_arrived(h, item, way, 4, way)

    def unit_of(u):
        turn = lax.rem(u, NX)
        return lax.rem(1 + 2 * turn + turn // 2, NX), u // NX

    def span_of(u):
        d, s = unit_of(u)
        return order[(at_x(d) * NZ + z) * SPANS + s]

    def find_places(part):
        span = lax.broadcasted_iota(jnp.int32, (1, NSPAN), 1)
        slot = (x - span // (SPANS * NZ) + NX) & (NX - 1)
        place = ((span // SPANS) & (NZ - 1)) * UNITS + slot * SPANS + (span & (SPANS - 1))
        loader = order_row[...]

        def some(i, carry):
            for n in range(8):
                t = (4 * part + i) * 8 + n
                places[PAD + t] = jnp.max(jnp.where(loader == t, place, 0))
            return carry

        lax.fori_loop(0, 4, some, 0)

    def run_units(step, events=()):
        def unit_step(u, carry):
            for when, event in events:
                pl.when(u == when)(event)
            step(u)
            return carry

        lax.fori_loop(0, UNITS, unit_step, 0)

    def find_starts(u):
        span = span_of(u)
        token = span * BLOCK + lax.broadcasted_iota(jnp.int32, (BLOCK, HEAD_DIM), 0)
        start = jnp.zeros((BLOCK, HEAD_DIM), jnp.int32)
        end = jnp.int32(0)
        for j in range(NDOC):
            end = end + lengths[j]
            start = jnp.where(token >= end, end, start)
        starts[u] = start - (span - PAD) * BLOCK

    lane = lax.broadcasted_iota(jnp.int32, (BLOCK, 128), 1)
    row = lax.broadcasted_iota(jnp.int32, (BLOCK, 128), 0)

    def window_of(h, item, u):
        span = span_of(u)
        return jnp.concatenate([kv[h][item][places[span + n]] for n in range(WIN)], 0)

    def weigh(h, u):
        d, s = unit_of(u)
        q_rows = q_buf[h, lax.rem(NX - d, NX), pl.ds(pl.multiple_of(s * BLOCK, BLOCK), BLOCK), :]
        q = jnp.concatenate([q_rows[:, g * HEAD_DIM : (g + 1) * HEAD_DIM] for g in range(GROUP)], 0)
        keys_here = window_of(h, 0, u)
        start = starts[u]
        tops = [jnp.full((BLOCK, 128), -jnp.inf, jnp.float32)] * GROUP
        for first in range(0, WIN * BLOCK, 256):
            width = min(256, WIN * BLOCK - first)
            block = lax.dot_general(
                q, keys_here[first : first + width], (((1,), (1,)), ((), ())),
                preferred_element_type=jnp.float32,
            )
            for c in range(0, width, 128):
                allowed = lane + (first + c) >= start
                if first + c + 128 == WIN * BLOCK:
                    allowed = allowed & (lane - BLOCK <= row)
                for g in range(GROUP):
                    part = block[g * BLOCK : (g + 1) * BLOCK, c : c + 128]
                    part = jnp.where(allowed, part, -jnp.inf)
                    tops[g] = jnp.maximum(tops[g], part)
                    scores[(first + c) // 128, g * BLOCK : (g + 1) * BLOCK, :] = part
        for g in range(GROUP):
            rows = slice(g * BLOCK, (g + 1) * BLOCK)
            top = jnp.max(tops[g], axis=1, keepdims=True)
            total = jnp.zeros((BLOCK, 128), jnp.float32)
            for c in range(WIN // 2):
                part = jnp.exp2((scores[c, rows, :] - top) * SCALE)
                total = total + part
                weights[u, c, rows, :] = part.astype(jnp.bfloat16)
            total = jnp.sum(total, axis=1, keepdims=True)
            totals[u, rows, :] = jnp.broadcast_to(total, (BLOCK, HEAD_DIM))

    def o_rows(h, xx, s):
        return out.at[
            pl.ds(pl.multiple_of(s * BLOCK, BLOCK), BLOCK),
            pl.ds(pl.multiple_of(xx * QW + h * GW, GW), GW),
        ]

    def o_source(h, d, s):
        return o_buf.at[h, d, pl.ds(pl.multiple_of(s * BLOCK, BLOCK), BLOCK), :]

    def o_copy(h, d, s):
        sem = o_recv.at[h, d, s]
        return send(o_source(h, d, s), o_rows(h, x, s), o_send.at[h, d, s], sem, seq_of(at_x(d), z))

    def o_own(h, s):
        return pltpu.make_async_copy(o_source(h, 0, s), o_rows(h, x, s), o_recv.at[h, 0, s])

    def send_unit(h, u):
        d, s = unit_of(u)

        @pl.when(d > 0)
        def _():
            o_copy(h, d, s).start()

        @pl.when(d == 0)
        def _():
            o_own(h, s).start()

    def mix(h, u):
        d, s = unit_of(u)
        rounded = jnp.concatenate([weights[u, c] for c in range(WIN // 2)], 1)
        mixed = jnp.dot(rounded, window_of(h, 1, u), preferred_element_type=jnp.float32)
        mixed = (mixed / totals[u]).astype(jnp.bfloat16)
        for g in range(GROUP):
            o_buf[
                h, d, pl.ds(pl.multiple_of(s * BLOCK, BLOCK), BLOCK),
                g * HEAD_DIM : (g + 1) * HEAD_DIM,
            ] = mixed[g * BLOCK : (g + 1) * BLOCK]

        @pl.when(u > 0)
        def _():
            send_unit(h, u - 1)

    def q_wait(h):
        for d in range(NX):
            arrived(q_buf.at[h, d], q_recv.at[h, d])

    def forward(*step):
        return lambda: z_forward(*step)

    z_start(0, 0)
    for n in range(PAD):
        places[n] = 0
    find_places(0)
    z_forward_both(0, 0, 2)
    find_places(1)
    z_forward_both(0, 0, 3)
    z_start(0, 1)
    find_places(2)
    z_forward(0, 0, 4, 0)
    run_units(find_starts)
    z_forward_both(0, 1, 2)
    find_places(3)
    z_finish(0, 0)
    q_wait(0)
    run_units(
        functools.partial(weigh, 0),
        [(1, forward(0, 1, 3, 0)), (4, forward(0, 1, 3, 1)), (5, lambda: z_start(1, 0))],
    )
    z_forward(0, 1, 4, 0)
    z_forward_both(1, 0, 2)
    z_finish(0, 1)
    run_units(
        functools.partial(mix, 0),
        [(4, forward(1, 0, 3, 0)), (8, forward(1, 0, 3, 1)), (9, lambda: z_start(1, 1))],
    )
    send_unit(0, UNITS - 1)
    z_forward(1, 0, 4, 0)
    z_forward_both(1, 1, 2)
    z_finish(1, 0)
    q_wait(1)
    run_units(
        functools.partial(weigh, 1),
        [(4, forward(1, 1, 3, 0)), (7, forward(1, 1, 3, 1)), (11, forward(1, 1, 4, 0))],
    )
    z_finish(1, 1)
    run_units(functools.partial(mix, 1))
    send_unit(1, UNITS - 1)

    for h in range(KVH):
        for s in range(SPANS):
            o_own(h, s).wait()
            for d in range(1, NX):
                o_copy(h, d, s).wait_send()
                arrived(o_rows(h, at_x(NX - d), s), o_recv.at[h, d, s])
    for h in range(KVH):
        for d in range(1, NX):
            for item in range(2):
                x_copy(h, item, d).wait_send()
            q_copy(h, d).wait_send()
        for item in range(2):
            for way in range(2):
                for d in range(NX):
                    z_own(h, item, way, d).wait_send()
                for half in range(2):
                    for hop in range(2, 5 if half == way else 4):
                        z_copy(h, item, way, hop, half).wait_send()


def shards(queries, keys, values, lengths, span_order):
    smem = pl.BlockSpec(memory_space=pltpu.SMEM)
    vmem = pl.BlockSpec(memory_space=pltpu.VMEM)
    anywhere = pl.BlockSpec(memory_space=pl.ANY)
    dma = pltpu.SemaphoreType.DMA
    return pl.pallas_call(
        body,
        out_shape=pltpu.VMEM((ROWS, HEADS * HEAD_DIM), jnp.bfloat16),
        in_specs=[smem, smem, vmem, anywhere, anywhere, anywhere],
        out_specs=vmem,
        scratch_shapes=[
            *[pltpu.VMEM((NSPAN, BLOCK, HEAD_DIM), jnp.bfloat16)] * (2 * KVH),
            pltpu.VMEM((KVH, NX, ROWS, GW), jnp.bfloat16),
            pltpu.VMEM((KVH, NX, ROWS, GW), jnp.bfloat16),
            pltpu.SMEM((PAD + NSPAN,), jnp.int32),
            pltpu.VMEM((UNITS, BLOCK, HEAD_DIM), jnp.int32),
            pltpu.VMEM((WIN // 2, GROUP * BLOCK, 128), jnp.float32),
            pltpu.VMEM((UNITS, WIN // 2, GROUP * BLOCK, 128), jnp.bfloat16),
            pltpu.VMEM((UNITS, GROUP * BLOCK, HEAD_DIM), jnp.float32),
            dma((KVH, 2, NX)),
            dma((KVH, 2, NX)),
            dma((KVH, NX)),
            dma((KVH, NX)),
            dma((KVH, 2, 2, NX)),
            dma((KVH, 2, 2, NX)),
            dma((KVH, 2, 2, 3, 2)),
            dma((KVH, 2, 2, 3, 2)),
            dma((KVH, NX, SPANS)),
            dma((KVH, NX, SPANS)),
        ],
        compiler_params=pltpu.CompilerParams(
            collective_id=0, has_side_effects=True, vmem_limit_bytes=58 * 2**20
        ),
        name="span_attention",
    )(
        lengths, span_order, span_order.reshape(1, NSPAN), queries,
        keys.reshape(SPANS, BLOCK, KV_HEADS * HEAD_DIM),
        values.reshape(SPANS, BLOCK, KV_HEADS * HEAD_DIM),
    )


def solution(mesh):
    placed = (
        P(("dp", "seq"), None),
        P(("dp", "seq"), None),
        P(("dp", "seq"), None),
        P("dp"),
        P("dp"),
    )
    return jax.shard_map(
        shards, mesh=mesh, in_specs=placed, out_specs=P(("dp", "seq"), None), check_vma=False
    )
```
